32 devices in a mesh: groups: 2 (over x), tensor: 8 (over z, y), dp: 2 (over core).
Axes of the slice: x: 2, y: 2, z: 4, core: 2. Of those that a mesh axis runs over, the one named last changes fastest.
Arguments:
- inputs: bfloat16 [512, 4096], P(('groups', 'tensor', 'dp')), parts along dimension 0, may hold values from -6 to 6
- cotangent: bfloat16 [512, 4096], P(('groups', 'tensor', 'dp')), parts along dimension 0, may hold values from -6 to 6
- gate_blocks: bfloat16 [4096, 8192], P(None, 'tensor'), may hold values from -0.09375 to 0.09375
- gate_scales: float32 [32, 64], P(None, 'tensor'), may hold values from 0.5 to 2
- up_blocks: bfloat16 [4096, 8192], P(None, 'tensor'), may hold values from -0.09375 to 0.09375
- up_scales: float32 [32, 64], P(None, 'tensor'), may hold values from 0.5 to 2
- down_blocks: bfloat16 [8192, 4096], P('tensor'), may hold values from -0.0625 to 0.0625
- down_scales: float32 [64, 32], P('tensor'), may hold values from 0.5 to 2
- first_stored: bfloat16 [8192, 4096], P(None, ('tensor', 'dp')), may hold values from -0.017944336 to 0.017944336
- second_stored: bfloat16 [8192, 4096], P(None, ('tensor', 'dp')), may hold values from 9.953976e-06 to 9.9658966e-05
- owner_map: int32 [16], replicated, may hold values from 0 to 15, each once
Outputs:
- input_grad: bfloat16 [512, 4096], P(('groups', 'tensor', 'dp')), parts along dimension 0
- update: bfloat16 [16384, 4096], P(('groups', 'tensor', 'dp')), parts along dimension 0
The draws below stay inside these ranges and needn't reach their ends.
There are 2 independent parts, one for each index of `groups`. The reference program is written for one: setup_inputs(seed, part) draws one part's arguments, and reference() takes and returns one part's arrays. A program takes and returns all parts, laid end to end along the dimension named above; an argument that names none is the same for every part. Nothing has to cross between parts.
Inputs may be any that keep to these rules, and one draw needn't show every extreme that they name: owner_map is a permutation of the numbers below 16.
All inputs are finite; a program needn't handle non-finite values.
Results may differ from the reference program's by a relative error of at most 0.012.
Values may be sent and summed in bfloat16 or wider, within the bound.
A program may use at most 192 MiB of HBM per device.

```python
import math
import jax
import jax.numpy as jnp
from jax import lax

D = 4096
FF = 8192
BLOCK = 128
TOKENS = 256
OWNERS = 16
N_TENSOR = 8


def steps_of(rng, extent, split, smallest, top_value):
    def one(dim, parts):
        steps = jax.random.uniform(jax.random.fold_in(jax.random.fold_in(rng, 6), dim), (parts,), jnp.float32, smallest / len(split), top_value / len(split))
        return jnp.repeat(jnp.exp(steps), extent[dim] // parts).reshape((-1,) + (1,) * (len(extent) - dim - 1))

    gain = one(*split[0])
    for cut in split[1:]:
        gain = gain * one(*cut)
    return gain


def gaussian(key, dims, scale, most, shards=(), held_as=jnp.bfloat16):
    drawn = scale * jax.random.normal(key, dims, jnp.float32)
    if shards:
        drawn = drawn * steps_of(key, dims, shards, -0.22, 0.18)
    return jnp.clip(drawn, -most, most).astype(held_as)


def setup_inputs(seed: int = 0, part: int = 0) -> dict:
    seeds = jax.random.split(jax.random.key(seed), 12)
    part_splits = jax.random.split(jax.random.fold_in(seeds[11], part), 12)
    return {
        "inputs": gaussian(part_splits[0], (TOKENS, D), 1.0, 6.0, ((0, 16),)),
        "cotangent": gaussian(part_splits[1], (TOKENS, D), 1.0, 6.0, ((0, 16),)),
        "gate_blocks": gaussian(seeds[2], (D, FF), D ** -0.5, 0.09375, ((1, 8),)),
        "gate_scales": jnp.clip(jnp.exp(math.log(2.0) - 1.3862944 * jax.random.uniform(seeds[3], (D // BLOCK, FF // BLOCK), jnp.float32) ** steps_of(seeds[3], (D // BLOCK, FF // BLOCK), ((1, 8),), -0.2, 0.2)), 0.5, 2.0),
        "up_blocks": gaussian(seeds[4], (D, FF), D ** -0.5, 0.09375, ((1, 8),)),
        "up_scales": jnp.clip(jnp.exp(math.log(2.0) - 1.3862944 * jax.random.uniform(seeds[5], (D // BLOCK, FF // BLOCK), jnp.float32) ** steps_of(seeds[5], (D // BLOCK, FF // BLOCK), ((1, 8),), -0.2, 0.2)), 0.5, 2.0),
        "down_blocks": gaussian(seeds[6], (FF, D), FF ** -0.5, 0.0625, ((0, 8),)),
        "down_scales": jnp.clip(jnp.exp(math.log(2.0) - 1.3862944 * jax.random.uniform(seeds[7], (FF // BLOCK, D // BLOCK), jnp.float32) ** steps_of(seeds[7], (FF // BLOCK, D // BLOCK), ((0, 8),), -0.2, 0.2)), 0.5, 2.0),
        "first_stored": gaussian(seeds[8], (FF, D), 0.003, 0.017944336, ((1, 16),)),
        "second_stored": jnp.clip(jnp.exp(math.log(9.965896606445312e-05) - 2.303782 * jax.random.uniform(seeds[9], (FF, D), jnp.float32) ** steps_of(seeds[9], (FF, D), ((1, 16),), -0.2, 0.2)), 9.953975677490234e-06, 9.965896606445312e-05).astype(jnp.bfloat16),
        "owner_map": jax.random.permutation(seeds[10], OWNERS).astype(jnp.int32),
    }


def dequantize(blocks, scales, tile):
    rows, cols = blocks.shape
    shaped = blocks.astype(jnp.float32).reshape(rows // tile, tile, cols // tile, tile)
    scaled = shaped * scales[:, None, :, None]
    return scaled.reshape(rows, cols).astype(jnp.bfloat16)

def silu_parts(gate_pre):
    sigma = jax.nn.sigmoid(gate_pre)
    return (gate_pre * sigma, sigma * (1.0 + gate_pre * (1.0 - sigma)))

def reference(inputs, cotangent, gate_blocks, gate_scales, up_blocks, up_scales, down_blocks, down_scales, first_stored, second_stored, owner_map):
    w_gate = dequantize(gate_blocks, gate_scales, BLOCK)
    w_up = dequantize(up_blocks, up_scales, BLOCK)
    w_down = dequantize(down_blocks, down_scales, BLOCK)
    gate_pre = jnp.dot(inputs, w_gate, preferred_element_type=jnp.float32)
    up_pre = jnp.dot(inputs, w_up, preferred_element_type=jnp.float32)
    activated, slope = silu_parts(gate_pre)
    hidden = (activated * up_pre).astype(jnp.bfloat16)
    back_hidden = lax.dot_general(cotangent, w_down, (((1,), (1,)), ((), ())), preferred_element_type=jnp.float32)
    grad_gate = (back_hidden * up_pre * slope).astype(jnp.bfloat16)
    grad_up = (back_hidden * activated).astype(jnp.bfloat16)
    units = FF // N_TENSOR

    def add_block(total, index):
        start = index * units
        gate_cols = lax.dynamic_slice_in_dim(grad_gate, start, units, 1)
        up_cols = lax.dynamic_slice_in_dim(grad_up, start, units, 1)
        wg_cols = lax.dynamic_slice_in_dim(w_gate, start, units, 1)
        wu_cols = lax.dynamic_slice_in_dim(w_up, start, units, 1)
        term = lax.dot_general(gate_cols, wg_cols, (((1,), (1,)), ((), ())), preferred_element_type=jnp.float32)
        term = term + lax.dot_general(up_cols, wu_cols, (((1,), (1,)), ((), ())), preferred_element_type=jnp.float32)
        rounded = lax.optimization_barrier(term.astype(jnp.bfloat16))
        return (total + rounded.astype(jnp.float32), None)
    start_total = jnp.zeros((TOKENS, D), jnp.float32)
    total, _ = lax.scan(add_block, start_total, jnp.arange(N_TENSOR, dtype=jnp.int32))
    input_grad = total.astype(jnp.bfloat16)
    grad_down = jnp.dot(hidden.T, cotangent, preferred_element_type=jnp.float32) / TOKENS
    width = D // OWNERS
    placement_of = jnp.zeros((OWNERS,), jnp.int32).at[owner_map].set(jnp.arange(OWNERS, dtype=jnp.int32))
    first_true = jnp.take(first_stored.reshape(FF, OWNERS, width), placement_of, axis=1).reshape(FF, D)
    second_true = jnp.take(second_stored.reshape(FF, OWNERS, width), placement_of, axis=1).reshape(FF, D)
    first_new = 0.9 * first_true.astype(jnp.float32) + 0.1 * grad_down
    second_new = 0.95 * second_true.astype(jnp.float32) + 0.05 * grad_down * grad_down
    update = (first_new / (jnp.sqrt(second_new) + 1e-08)).astype(jnp.bfloat16)
    return (input_grad, update)
```

```python
import functools

import jax
import jax.numpy as jnp
from jax import lax
from jax.experimental import pallas as pl
from jax.experimental.pallas import tpu as pltpu
from jax.sharding import PartitionSpec as P

BLOCK = 128
CHUNKS = 4
TOKENS_AXES = ("tensor", "dp")


def dequantize(blocks, scales, tile):
    rows, cols = blocks.shape
    shaped = blocks.astype(jnp.float32).reshape(rows // tile, tile, cols // tile, tile)
    scaled = shaped * scales[:, None, :, None]
    return scaled.reshape(rows, cols).astype(jnp.bfloat16)


def silu_parts(gate_pre):
    sigma = jax.nn.sigmoid(gate_pre)
    return (gate_pre * sigma, sigma * (1.0 + gate_pre * (1.0 - sigma)))


def adam(first, second, grad):
    first_new = 0.9 * first.astype(jnp.float32) + 0.1 * grad
    second_new = 0.95 * second.astype(jnp.float32) + 0.05 * grad * grad
    return (first_new / (jnp.sqrt(second_new) + 1e-08)).astype(jnp.bfloat16)


def adam_kernel(tokens, owner_ref, side_ref, hidden_ref, cot_ref, mine_ref, other_ref, *rest):
    out_ref = rest[-1]
    even = side_ref[0] == 0
    grad = (
        jnp.dot(hidden_ref[...], cot_ref[...], preferred_element_type=jnp.float32) / tokens
    )
    mine = mine_ref[0].astype(jnp.float32)
    other = other_ref[0].astype(jnp.float32)
    first = jnp.where(even, mine, other)
    second = jnp.where(even, other, mine)
    out_ref[...] = adam(first, second, grad)


def adam_chunk(index, chunks, owner_map, side, hidden_t, cot, mine, other, out):
    owners, rows, width = mine.shape
    units, tokens = hidden_t.shape
    cols = cot.shape[1]
    in_specs = [
        pl.BlockSpec((rows, tokens), lambda j, o, s: (index, 0)),
        pl.BlockSpec((tokens, width), lambda j, o, s: (0, o[j])),
        pl.BlockSpec((1, rows, width), lambda j, o, s: (j, 0, 0)),
        pl.BlockSpec((1, rows, width), lambda j, o, s: (j, 0, 0)),
    ]
    args = [owner_map, side, hidden_t, cot, mine, other]
    aliases = {}
    if out is not None:
        in_specs.append(pl.BlockSpec(memory_space=pl.ANY))
        args.append(out)
        aliases = {len(args) - 1: 0}
    return pl.pallas_call(
        functools.partial(adam_kernel, tokens),
        grid_spec=pltpu.PrefetchScalarGridSpec(
            num_scalar_prefetch=2,
            grid=(owners,),
            in_specs=in_specs,
            out_specs=pl.BlockSpec((rows, width), lambda j, o, s: (index, o[j])),
        ),
        out_shape=jax.ShapeDtypeStruct((units, cols), jnp.bfloat16),
        input_output_aliases=aliases,
        cost_estimate=pl.CostEstimate(
            flops=2 * rows * tokens * cols,
            bytes_accessed=2 * rows * cols * 3 + 2 * tokens * cols,
            transcendentals=0,
        ),
        name="adam",
    )(*args)


def body(
    inputs,
    cotangent,
    gate_blocks,
    gate_scales,
    up_blocks,
    up_scales,
    down_blocks,
    down_scales,
    first_stored,
    second_stored,
    owner_map,
):
    group = lax.axis_index("groups")
    half_id = lax.axis_index("dp")
    group_count = lax.axis_size("groups")
    dp_count = lax.axis_size("dp")
    owners = lax.axis_size("tensor") * dp_count
    paired = group_count % 2 == 0
    ff, width = first_stored.shape
    rows = ff // owners
    side = lax.rem(group, 2)

    x_all = lax.all_gather(inputs, TOKENS_AXES, axis=0, tiled=True)
    cot = lax.all_gather(cotangent, TOKENS_AXES, axis=0, tiled=True)

    chunks = CHUNKS if rows % (CHUNKS * 16) == 0 else 1
    step = rows // chunks
    shaped_first = first_stored.reshape(owners, chunks, step, width)
    shaped_second = second_stored.reshape(owners, chunks, step, width)
    swap = [(i, i ^ 1) for i in range(group_count)]
    received = []
    for c in range(chunks):
        if paired:
            picked = jnp.where(side == 0, shaped_first[:, c], shaped_second[:, c])
            mine = lax.all_to_all(picked, TOKENS_AXES, split_axis=0, concat_axis=0, tiled=True)
            received.append((mine, lax.ppermute(mine, "groups", swap)))
        else:
            received.append(
                tuple(
                    lax.all_to_all(a[:, c], TOKENS_AXES, split_axis=0, concat_axis=0, tiled=True)
                    for a in (shaped_first, shaped_second)
                )
            )

    units = gate_blocks.shape[1] // dp_count
    tiles = units // BLOCK
    cut = lambda a, size, dim: lax.dynamic_slice_in_dim(a, half_id * size, size, dim)
    w_gate = dequantize(cut(gate_blocks, units, 1), cut(gate_scales, tiles, 1), BLOCK)
    w_up = dequantize(cut(up_blocks, units, 1), cut(up_scales, tiles, 1), BLOCK)
    w_down = dequantize(cut(down_blocks, units, 0), cut(down_scales, tiles, 0), BLOCK)

    gate_pre = jnp.dot(x_all, w_gate, preferred_element_type=jnp.float32)
    up_pre = jnp.dot(x_all, w_up, preferred_element_type=jnp.float32)
    activated, slope = silu_parts(gate_pre)
    hidden = (activated * up_pre).astype(jnp.bfloat16)
    back_hidden = lax.dot_general(
        cot, w_down, (((1,), (1,)), ((), ())), preferred_element_type=jnp.float32
    )
    grad_gate = (back_hidden * up_pre * slope).astype(jnp.bfloat16)
    grad_up = (back_hidden * activated).astype(jnp.bfloat16)
    nt = (((1,), (1,)), ((), ()))
    partial = lax.dot_general(grad_gate, w_gate, nt, preferred_element_type=jnp.float32)
    partial = partial + lax.dot_general(grad_up, w_up, nt, preferred_element_type=jnp.float32)
    input_grad = lax.psum_scatter(
        partial.astype(jnp.bfloat16), TOKENS_AXES, scatter_dimension=0, tiled=True
    )

    hidden_t = hidden.T
    if width % 128 == 0 and step % 16 == 0:
        sides = jnp.full((1,), side if paired else 0, jnp.int32)
        update = None
        for c, (mine, other) in enumerate(received):
            update = adam_chunk(
                c, chunks, owner_map, sides, hidden_t, cot, mine, other, update
            )
    else:
        grad = jnp.dot(hidden_t, cot, preferred_element_type=jnp.float32) / cot.shape[0]
        placement = jnp.zeros((owners,), jnp.int32).at[owner_map].set(
            jnp.arange(owners, dtype=jnp.int32)
        )
        parts = []
        for c, (mine, other) in enumerate(received):
            if paired:
                first = jnp.where(side == 0, mine, other)
                second = jnp.where(side == 0, other, mine)
            else:
                first, second = mine, other
            lay = lambda a: jnp.take(a, placement, axis=0).swapaxes(0, 1).reshape(step, -1)
            parts.append(adam(lay(first), lay(second), grad[c * step : (c + 1) * step]))
        update = jnp.concatenate(parts, axis=0)
    return (input_grad, update)


def solution(mesh):
    return jax.shard_map(
        body,
        mesh=mesh,
        in_specs=(
            P(("groups", "tensor", "dp"), None),
            P(("groups", "tensor", "dp"), None),
            P(None, "tensor"),
            P(None, "tensor"),
            P(None, "tensor"),
            P(None, "tensor"),
            P("tensor", None),
            P("tensor", None),
            P(None, ("tensor", "dp")),
            P(None, ("tensor", "dp")),
            P(),
        ),
        out_specs=(P(("groups", "tensor", "dp"), None), P(("groups", "tensor", "dp"), None)),
        check_vma=False,
    )
```

```python
import functools

import jax
import jax.numpy as jnp
from jax import lax
from jax.experimental import pallas as pl
from jax.experimental.pallas import tpu as pltpu
from jax.sharding import PartitionSpec as P

BLOCK = 128
CHUNKS = 4
TOKENS_AXES = ("tensor", "dp")


def dequantize(blocks, scales, tile):
    rows, cols = blocks.shape
    shaped = blocks.astype(jnp.float32).reshape(rows // tile, tile, cols // tile, tile)
    scaled = shaped * scales[:, None, :, None]
    return scaled.reshape(rows, cols).astype(jnp.bfloat16)


def silu_parts(gate_pre):
    sigma = jax.nn.sigmoid(gate_pre)
    return (gate_pre * sigma, sigma * (1.0 + gate_pre * (1.0 - sigma)))


def adam(first, second, grad):
    first_new = 0.9 * first.astype(jnp.float32) + 0.1 * grad
    second_new = 0.95 * second.astype(jnp.float32) + 0.05 * grad * grad
    return (first_new / (jnp.sqrt(second_new) + 1e-08)).astype(jnp.bfloat16)


def adam_kernel(tokens, owner_ref, side_ref, hidden_ref, cot_ref, mine_ref, other_ref, *rest):
    out_ref = rest[-1]
    owners, _, width = mine_ref.shape
    even = side_ref[0] == 0

    @pl.loop(0, owners)
    def _(j):
        columns = pl.ds(pl.multiple_of(owner_ref[j] * width, width), width)
        grad = (
            jnp.dot(hidden_ref[...], cot_ref[:, columns], preferred_element_type=jnp.float32)
            / tokens
        )
        mine = mine_ref[j].astype(jnp.float32)
        other = other_ref[j].astype(jnp.float32)
        first = jnp.where(even, mine, other)
        second = jnp.where(even, other, mine)
        out_ref[:, columns] = adam(first, second, grad)


def adam_chunk(index, owner_map, side, hidden_t, cot, mine, other, out):
    owners, rows, width = mine.shape
    units, tokens = hidden_t.shape
    cols = cot.shape[1]
    in_specs = [
        pl.BlockSpec((rows, tokens), lambda i, o, s: (index, 0)),
        pl.BlockSpec((tokens, cols), lambda i, o, s: (0, 0)),
        pl.BlockSpec((owners, rows, width), lambda i, o, s: (0, 0, 0)),
        pl.BlockSpec((owners, rows, width), lambda i, o, s: (0, 0, 0)),
    ]
    args = [owner_map, side, hidden_t, cot, mine, other]
    aliases = {}
    if out is not None:
        in_specs.append(pl.BlockSpec(memory_space=pl.ANY))
        args.append(out)
        aliases = {len(args) - 1: 0}
    return pl.pallas_call(
        functools.partial(adam_kernel, tokens),
        grid_spec=pltpu.PrefetchScalarGridSpec(
            num_scalar_prefetch=2,
            grid=(1,),
            in_specs=in_specs,
            out_specs=pl.BlockSpec((rows, cols), lambda i, o, s: (index, 0)),
        ),
        out_shape=jax.ShapeDtypeStruct((units, cols), jnp.bfloat16),
        input_output_aliases=aliases,
        cost_estimate=pl.CostEstimate(
            flops=2 * rows * tokens * cols,
            bytes_accessed=2 * rows * cols * 3 + 2 * tokens * cols,
            transcendentals=0,
        ),
        name="adam",
    )(*args)


MESH = pl.DeviceIdType.MESH
LOW = 2


def place():
    group = lax.axis_index("groups")
    tensor = lax.axis_index("tensor")
    core = lax.axis_index("dp")
    high, low = tensor // LOW, lax.rem(tensor, LOW)
    return group, high, low, core


def greet(highs):
    group, high, low, core = place()
    barrier = pltpu.get_barrier_semaphore()
    peers = [(group, lax.rem(high + r, highs) * LOW + low, core) for r in range(1, highs)]
    peers.append((group, high * LOW + 1 - low, core))
    peers.append((group, high * LOW + low, 1 - core))
    for peer in peers:
        pl.semaphore_signal(barrier, inc=1, device_id=peer, device_id_type=MESH)
    pl.semaphore_wait(barrier, len(peers))


def gather_kernel(highs, x_ref, c_ref, x_out, c_out, send_sem, recv_sem, local_sem):
    group, high, low, core = place()
    pairs = ((x_ref, x_out), (c_ref, c_out))
    block = lambda h, l, k: (h * LOW + l) * 2 + k
    me = block(high, low, core)
    greet(highs)
    started = []

    def push(arr, source, slot, target):
        copy = pltpu.make_async_remote_copy(
            src_ref=source,
            dst_ref=pairs[arr][1].at[slot],
            send_sem=send_sem.at[len(started)],
            recv_sem=recv_sem.at[slot, arr],
            device_id=target,
            device_id_type=MESH,
        )
        copy.start()
        started.append(copy)

    def arrive(arr, slot):
        ref = pairs[arr][1].at[slot]
        pltpu.make_async_remote_copy(
            src_ref=ref,
            dst_ref=ref,
            send_sem=send_sem.at[0],
            recv_sem=recv_sem.at[slot, arr],
            device_id=(group, high * LOW + low, 1 - core),
            device_id_type=MESH,
        ).wait_recv()

    across = (group, high * LOW + 1 - low, core)
    sibling = (group, high * LOW + low, 1 - core)
    locals_ = []
    for arr, (source, out) in enumerate(pairs):
        for r in range(1, highs):
            push(arr, source, me, (group, lax.rem(high + r, highs) * LOW + low, core))
        push(arr, source, me, across)
        push(arr, source, me, sibling)
        keep = pltpu.make_async_copy(source, out.at[me], local_sem.at[arr])
        keep.start()
        locals_.append(keep)
    for arr, (_, out) in enumerate(pairs):
        for r in range(highs - 1, 0, -1):
            slot = block(lax.rem(high + r, highs), low, core)
            arrive(arr, slot)
            push(arr, out.at[slot], slot, across)
            push(arr, out.at[slot], slot, sibling)
        for r in range(highs, 0, -1):
            slot = block(lax.rem(high + r, highs), 1 - low, core)
            arrive(arr, slot)
            push(arr, out.at[slot], slot, sibling)
    for arr in range(2):
        for h in range(highs):
            for l in range(LOW):
                arrive(arr, block(h, l, 1 - core))
    for keep in locals_:
        keep.wait()
    for copy in started:
        copy.wait_send()


def gather_tokens(x, c):
    tensor_count = lax.axis_size("tensor")
    highs = tensor_count // LOW
    rows, cols = x.shape
    slots = tensor_count * 2
    pushes = 2 * (highs + 1 + 2 * (highs - 1) + highs)
    full = jax.ShapeDtypeStruct((slots, rows, cols), x.dtype)
    vmem = pl.BlockSpec(memory_space=pltpu.VMEM)
    x_all, c_all = pl.pallas_call(
        functools.partial(gather_kernel, highs),
        out_shape=(full, full),
        in_specs=[vmem, vmem],
        out_specs=(vmem, vmem),
        scratch_shapes=[
            pltpu.SemaphoreType.DMA((pushes,)),
            pltpu.SemaphoreType.DMA((slots, 2)),
            pltpu.SemaphoreType.DMA((2,)),
        ],
        compiler_params=pltpu.CompilerParams(collective_id=0, has_side_effects=True),
        cost_estimate=pl.CostEstimate(flops=0, bytes_accessed=60_000_000, transcendentals=0),
        name="gather_tokens",
    )(x, c)
    return x_all.reshape(slots * rows, cols), c_all.reshape(slots * rows, cols)


def scatter_kernel(
    highs, p_ref, o_ref, got_a, sum_a, got_b, sum_b, got_c,
    send_a, recv_a, send_b, recv_b, send_c, recv_c,
):
    group, high, low, core = place()
    across = (group, high * LOW + 1 - low, core)
    sibling = (group, high * LOW + low, 1 - core)
    greet(highs)
    add = lambda a, b: (a.astype(jnp.float32) + b.astype(jnp.float32)).astype(jnp.bfloat16)

    def copy_to(source, target_ref, send, recv, target):
        return pltpu.make_async_remote_copy(
            src_ref=source,
            dst_ref=target_ref,
            send_sem=send,
            recv_sem=recv,
            device_id=target,
            device_id_type=MESH,
        )

    order = []
    for l in (1 - low, low):
        for r in range(1, highs + 1):
            order.append((lax.rem(high + r, highs), l))
    first = []
    for k, (h, l) in enumerate(order):
        t = h * LOW + l
        copy = copy_to(p_ref.at[t * 2 + 1 - core], got_a.at[k], send_a.at[k], recv_a.at[k], sibling)
        copy.start()
        first.append(copy)
    second = []
    for k, (h, l) in enumerate(order):
        t = h * LOW + l
        first[k].wait_recv()
        sum_a[k] = add(p_ref[t * 2 + core], got_a[k])
        if k < highs:
            copy = copy_to(sum_a.at[k], got_b.at[k], send_b.at[k], recv_b.at[k], across)
            copy.start()
            second.append(copy)
    third = []
    for r in range(1, highs + 1):
        k = r - 1
        second[k].wait_recv()
        sum_b[k] = add(sum_a[highs + k], got_b[k])
        if r < highs:
            copy = copy_to(
                sum_b.at[k],
                got_c.at[k],
                send_c.at[k],
                recv_c.at[k],
                (group, lax.rem(high + r, highs) * LOW + low, core),
            )
            copy.start()
            third.append(copy)
    total = sum_b[highs - 1].astype(jnp.float32)
    for k, copy in enumerate(third):
        copy.wait_recv()
        total = total + got_c[k].astype(jnp.float32)
    o_ref[...] = total.astype(jnp.bfloat16)
    for copy in first + second + third:
        copy.wait_send()


def scatter_sum(partial):
    tensor_count = lax.axis_size("tensor")
    highs = tensor_count // LOW
    slots = tensor_count * 2
    rows, cols = partial.shape[0] // slots, partial.shape[1]
    vmem = pl.BlockSpec(memory_space=pltpu.VMEM)
    buf = lambda count: pltpu.VMEM((count, rows, cols), jnp.bfloat16)
    sem = pltpu.SemaphoreType.DMA
    return pl.pallas_call(
        functools.partial(scatter_kernel, highs),
        out_shape=jax.ShapeDtypeStruct((rows, cols), jnp.bfloat16),
        in_specs=[vmem],
        out_specs=vmem,
        scratch_shapes=[
            buf(tensor_count), buf(tensor_count), buf(highs), buf(highs), buf(highs - 1),
            sem((tensor_count,)), sem((tensor_count,)), sem((highs,)), sem((highs,)),
            sem((highs - 1,)), sem((highs - 1,)),
        ],
        compiler_params=pltpu.CompilerParams(collective_id=1, has_side_effects=True),
        cost_estimate=pl.CostEstimate(flops=0, bytes_accessed=60_000_000, transcendentals=0),
        name="scatter_sum",
    )(partial.reshape(slots, rows, cols))


def step_of(
    inputs,
    cotangent,
    gate_blocks,
    gate_scales,
    up_blocks,
    up_scales,
    down_blocks,
    down_scales,
    first_stored,
    second_stored,
    owner_map,
):
    group = lax.axis_index("groups")
    half_id = lax.axis_index("dp")
    group_count = lax.axis_size("groups")
    dp_count = lax.axis_size("dp")
    owners = lax.axis_size("tensor") * dp_count
    paired = group_count % 2 == 0
    ff, width = first_stored.shape
    rows = ff // owners
    side = lax.rem(group, 2)

    own_kernels = dp_count == 2 and owners <= 16 and owners % 8 == 0 and inputs.shape[0] % 16 == 0
    if own_kernels:
        x_all, cot = gather_tokens(inputs, cotangent)
    else:
        x_all = lax.all_gather(inputs, TOKENS_AXES, axis=0, tiled=True)
        cot = lax.all_gather(cotangent, TOKENS_AXES, axis=0, tiled=True)

    chunks = CHUNKS if rows % (CHUNKS * 16) == 0 else 1
    step = rows // chunks
    shaped_first = first_stored.reshape(owners, chunks, step, width)
    shaped_second = second_stored.reshape(owners, chunks, step, width)
    swap = [(i, i ^ 1) for i in range(group_count)]
    received = []
    for c in range(chunks):
        if paired:
            picked = jnp.where(side == 0, shaped_first[:, c], shaped_second[:, c])
            if c == 1:
                picked, x_all, cot = lax.optimization_barrier((picked, x_all, cot))
            mine = lax.all_to_all(picked, TOKENS_AXES, split_axis=0, concat_axis=0, tiled=True)
            other = lax.ppermute(mine, "groups", swap)
            received.append((mine, other))
        else:
            received.append(
                tuple(
                    lax.all_to_all(a[:, c], TOKENS_AXES, split_axis=0, concat_axis=0, tiled=True)
                    for a in (shaped_first, shaped_second)
                )
            )

    units = gate_blocks.shape[1] // dp_count
    tiles = units // BLOCK
    cut = lambda a, size, dim: lax.dynamic_slice_in_dim(a, half_id * size, size, dim)
    w_gate = dequantize(cut(gate_blocks, units, 1), cut(gate_scales, tiles, 1), BLOCK)
    w_up = dequantize(cut(up_blocks, units, 1), cut(up_scales, tiles, 1), BLOCK)
    w_down = dequantize(cut(down_blocks, units, 0), cut(down_scales, tiles, 0), BLOCK)

    gate_pre = jnp.dot(x_all, w_gate, preferred_element_type=jnp.float32)
    up_pre = jnp.dot(x_all, w_up, preferred_element_type=jnp.float32)
    activated, slope = silu_parts(gate_pre)
    hidden = (activated * up_pre).astype(jnp.bfloat16)
    back_hidden = lax.dot_general(
        cot, w_down, (((1,), (1,)), ((), ())), preferred_element_type=jnp.float32
    )
    grad_gate = (back_hidden * up_pre * slope).astype(jnp.bfloat16)
    grad_up = (back_hidden * activated).astype(jnp.bfloat16)
    nt = (((1,), (1,)), ((), ()))
    partial = lax.dot_general(grad_gate, w_gate, nt, preferred_element_type=jnp.float32)
    partial = partial + lax.dot_general(grad_up, w_up, nt, preferred_element_type=jnp.float32)
    partial = partial.astype(jnp.bfloat16)
    if own_kernels:
        input_grad = scatter_sum(partial)
    else:
        input_grad = lax.psum_scatter(partial, TOKENS_AXES, scatter_dimension=0, tiled=True)

    hidden_t = hidden.T
    if width % 128 == 0 and step % 16 == 0:
        sides = jnp.full((1,), side if paired else 0, jnp.int32)
        update = None
        for c, (mine, other) in enumerate(received):
            update = adam_chunk(c, owner_map, sides, hidden_t, cot, mine, other, update)
    else:
        grad = jnp.dot(hidden_t, cot, preferred_element_type=jnp.float32) / cot.shape[0]
        placement = jnp.zeros((owners,), jnp.int32).at[owner_map].set(
            jnp.arange(owners, dtype=jnp.int32)
        )
        parts = []
        for c, (mine, other) in enumerate(received):
            if paired:
                first = jnp.where(side == 0, mine, other)
                second = jnp.where(side == 0, other, mine)
            else:
                first, second = mine, other
            lay = lambda a: jnp.take(a, placement, axis=0).swapaxes(0, 1).reshape(step, -1)
            parts.append(adam(lay(first), lay(second), grad[c * step : (c + 1) * step]))
        update = jnp.concatenate(parts, axis=0)
    return (input_grad, update)


def solution(mesh):
    return step_on(mesh)


def step_on(mesh):
    return jax.shard_map(
        step_of,
        mesh=mesh,
        in_specs=(
            P(("groups", "tensor", "dp"), None),
            P(("groups", "tensor", "dp"), None),
            P(None, "tensor"),
            P(None, "tensor"),
            P(None, "tensor"),
            P(None, "tensor"),
            P("tensor", None),
            P("tensor", None),
            P(None, ("tensor", "dp")),
            P(None, ("tensor", "dp")),
            P(),
        ),
        out_specs=(P(("groups", "tensor", "dp"), None), P(("groups", "tensor", "dp"), None)),
        check_vma=False,
    )
```

```python
import functools

import jax
import jax.numpy as jnp
from jax import lax
from jax.experimental import pallas as pl
from jax.experimental.pallas import tpu as pltpu
from jax.sharding import PartitionSpec as P

BLOCK = 128
SHARES = (4, 2, 1, 1)
TOKENS_AXES = ("tensor", "dp")


def dequantize(blocks, scales, tile):
    rows, cols = blocks.shape
    shaped = blocks.astype(jnp.float32).reshape(rows // tile, tile, cols // tile, tile)
    scaled = shaped * scales[:, None, :, None]
    return scaled.reshape(rows, cols).astype(jnp.bfloat16)


def silu_parts(gate_pre):
    sigma = jax.nn.sigmoid(gate_pre)
    return (gate_pre * sigma, sigma * (1.0 + gate_pre * (1.0 - sigma)))


def adam(first, second, grad):
    first_new = 0.9 * first.astype(jnp.float32) + 0.1 * grad
    second_new = 0.95 * second.astype(jnp.float32) + 0.05 * grad * grad
    return (first_new / (jnp.sqrt(second_new) + 1e-08)).astype(jnp.bfloat16)


def adam_kernel(owner_ref, side_ref, grad_ref, mine_ref, other_ref, *rest):
    out_ref = rest[-1]
    owners, _, width = mine_ref.shape
    even = side_ref[0] == 0

    @pl.loop(0, owners)
    def _(j):
        columns = pl.ds(pl.multiple_of(owner_ref[j] * width, width), width)
        mine = mine_ref[j].astype(jnp.float32)
        other = other_ref[j].astype(jnp.float32)
        first = jnp.where(even, mine, other)
        second = jnp.where(even, other, mine)
        out_ref[:, columns] = adam(first, second, grad_ref[:, columns])


def adam_chunk(start, step, owner_map, side, grad, mine, other, out):
    owners, rows, width = mine.shape
    units, cols = grad.shape
    base = start // step
    in_specs = [
        pl.BlockSpec((step, cols), lambda i, o, s: (base + i, 0)),
        pl.BlockSpec((owners, step, width), lambda i, o, s: (0, i, 0)),
        pl.BlockSpec((owners, step, width), lambda i, o, s: (0, i, 0)),
    ]
    args = [owner_map, side, grad, mine, other]
    aliases = {}
    if out is not None:
        in_specs.append(pl.BlockSpec(memory_space=pl.ANY))
        args.append(out)
        aliases = {len(args) - 1: 0}
    return pl.pallas_call(
        adam_kernel,
        grid_spec=pltpu.PrefetchScalarGridSpec(
            num_scalar_prefetch=2,
            grid=(rows // step,),
            in_specs=in_specs,
            out_specs=pl.BlockSpec((step, cols), lambda i, o, s: (base + i, 0)),
        ),
        out_shape=jax.ShapeDtypeStruct((units, cols), jnp.bfloat16),
        input_output_aliases=aliases,
        cost_estimate=pl.CostEstimate(
            flops=20 * rows * cols, bytes_accessed=10 * rows * cols, transcendentals=0
        ),
        name="adam",
    )(*args)


MESH = pl.DeviceIdType.MESH
LOW = 2


def place():
    group = lax.axis_index("groups")
    tensor = lax.axis_index("tensor")
    core = lax.axis_index("dp")
    high, low = tensor // LOW, lax.rem(tensor, LOW)
    return group, high, low, core


def greet(highs):
    group, high, low, core = place()
    barrier = pltpu.get_barrier_semaphore()
    peers = [(group, lax.rem(high + r, highs) * LOW + low, core) for r in range(1, highs)]
    peers.append((group, high * LOW + 1 - low, core))
    peers.append((group, high * LOW + low, 1 - core))
    for peer in peers:
        pl.semaphore_signal(barrier, inc=1, device_id=peer, device_id_type=MESH)
    pl.semaphore_wait(barrier, len(peers))


def gather_kernel(highs, x_ref, c_ref, x_out, c_out, send_sem, recv_sem, local_sem):
    group, high, low, core = place()
    pairs = ((x_ref, x_out), (c_ref, c_out))
    block = lambda h, l, k: (h * LOW + l) * 2 + k
    me = block(high, low, core)
    greet(highs)
    started = []

    def push(arr, source, slot, target):
        copy = pltpu.make_async_remote_copy(
            src_ref=source,
            dst_ref=pairs[arr][1].at[slot],
            send_sem=send_sem.at[len(started)],
            recv_sem=recv_sem.at[slot, arr],
            device_id=target,
            device_id_type=MESH,
        )
        copy.start()
        started.append(copy)

    def arrive(arr, slot):
        ref = pairs[arr][1].at[slot]
        pltpu.make_async_remote_copy(
            src_ref=ref,
            dst_ref=ref,
            send_sem=send_sem.at[0],
            recv_sem=recv_sem.at[slot, arr],
            device_id=(group, high * LOW + low, 1 - core),
            device_id_type=MESH,
        ).wait_recv()

    across = (group, high * LOW + 1 - low, core)
    sibling = (group, high * LOW + low, 1 - core)
    locals_ = []
    for arr, (source, out) in enumerate(pairs):
        for r in range(1, highs):
            push(arr, source, me, (group, lax.rem(high + r, highs) * LOW + low, core))
        push(arr, source, me, across)
        push(arr, source, me, sibling)
        keep = pltpu.make_async_copy(source, out.at[me], local_sem.at[arr])
        keep.start()
        locals_.append(keep)
    for arr, (_, out) in enumerate(pairs):
        for r in range(highs - 1, 0, -1):
            slot = block(lax.rem(high + r, highs), low, core)
            arrive(arr, slot)
            push(arr, out.at[slot], slot, across)
            push(arr, out.at[slot], slot, sibling)
        for r in range(highs, 0, -1):
            slot = block(lax.rem(high + r, highs), 1 - low, core)
            arrive(arr, slot)
            push(arr, out.at[slot], slot, sibling)
    for arr in range(2):
        for h in range(highs):
            for l in range(LOW):
                arrive(arr, block(h, l, 1 - core))
    for keep in locals_:
        keep.wait()
    for copy in started:
        copy.wait_send()


def gather_tokens(x, c):
    tensor_count = lax.axis_size("tensor")
    highs = tensor_count // LOW
    rows, cols = x.shape
    slots = tensor_count * 2
    pushes = 2 * (highs + 1 + 2 * (highs - 1) + highs)
    full = jax.ShapeDtypeStruct((slots, rows, cols), x.dtype)
    vmem = pl.BlockSpec(memory_space=pltpu.VMEM)
    x_all, c_all = pl.pallas_call(
        functools.partial(gather_kernel, highs),
        out_shape=(full, full),
        in_specs=[vmem, vmem],
        out_specs=(vmem, vmem),
        scratch_shapes=[
            pltpu.SemaphoreType.DMA((pushes,)),
            pltpu.SemaphoreType.DMA((slots, 2)),
            pltpu.SemaphoreType.DMA((2,)),
        ],
        compiler_params=pltpu.CompilerParams(collective_id=0, has_side_effects=True),
        cost_estimate=pl.CostEstimate(flops=0, bytes_accessed=60_000_000, transcendentals=0),
        name="gather_tokens",
    )(x, c)
    return x_all.reshape(slots * rows, cols), c_all.reshape(slots * rows, cols)


def scatter_kernel(
    highs, p_ref, o_ref, got_a, sum_a, got_b, sum_b, got_c,
    send_a, recv_a, send_b, recv_b, send_c, recv_c,
):
    group, high, low, core = place()
    across = (group, high * LOW + 1 - low, core)
    sibling = (group, high * LOW + low, 1 - core)
    greet(highs)
    add = lambda a, b: (a.astype(jnp.float32) + b.astype(jnp.float32)).astype(jnp.bfloat16)

    def copy_to(source, target_ref, send, recv, target):
        return pltpu.make_async_remote_copy(
            src_ref=source,
            dst_ref=target_ref,
            send_sem=send,
            recv_sem=recv,
            device_id=target,
            device_id_type=MESH,
        )

    order = []
    for l in (1 - low, low):
        for r in range(1, highs + 1):
            order.append((lax.rem(high + r, highs), l))
    first = []
    for k, (h, l) in enumerate(order):
        t = h * LOW + l
        copy = copy_to(p_ref.at[t * 2 + 1 - core], got_a.at[k], send_a.at[k], recv_a.at[k], sibling)
        copy.start()
        first.append(copy)
    second = []
    for k, (h, l) in enumerate(order):
        t = h * LOW + l
        first[k].wait_recv()
        sum_a[k] = add(p_ref[t * 2 + core], got_a[k])
        if k < highs:
            copy = copy_to(sum_a.at[k], got_b.at[k], send_b.at[k], recv_b.at[k], across)
            copy.start()
            second.append(copy)
    third = []
    for r in range(1, highs + 1):
        k = r - 1
        second[k].wait_recv()
        sum_b[k] = add(sum_a[highs + k], got_b[k])
        if r < highs:
            copy = copy_to(
                sum_b.at[k],
                got_c.at[k],
                send_c.at[k],
                recv_c.at[k],
                (group, lax.rem(high + r, highs) * LOW + low, core),
            )
            copy.start()
            third.append(copy)
    total = sum_b[highs - 1].astype(jnp.float32)
    for k, copy in enumerate(third):
        copy.wait_recv()
        total = total + got_c[k].astype(jnp.float32)
    o_ref[...] = total.astype(jnp.bfloat16)
    for copy in first + second + third:
        copy.wait_send()


def scatter_sum(partial):
    tensor_count = lax.axis_size("tensor")
    highs = tensor_count // LOW
    slots = tensor_count * 2
    rows, cols = partial.shape[0] // slots, partial.shape[1]
    vmem = pl.BlockSpec(memory_space=pltpu.VMEM)
    buf = lambda count: pltpu.VMEM((count, rows, cols), jnp.bfloat16)
    sem = pltpu.SemaphoreType.DMA
    return pl.pallas_call(
        functools.partial(scatter_kernel, highs),
        out_shape=jax.ShapeDtypeStruct((rows, cols), jnp.bfloat16),
        in_specs=[vmem],
        out_specs=vmem,
        scratch_shapes=[
            buf(tensor_count), buf(tensor_count), buf(highs), buf(highs), buf(highs - 1),
            sem((tensor_count,)), sem((tensor_count,)), sem((highs,)), sem((highs,)),
            sem((highs - 1,)), sem((highs - 1,)),
        ],
        compiler_params=pltpu.CompilerParams(collective_id=1, has_side_effects=True),
        cost_estimate=pl.CostEstimate(flops=0, bytes_accessed=60_000_000, transcendentals=0),
        name="scatter_sum",
    )(partial.reshape(slots, rows, cols))


def step_of(
    inputs,
    cotangent,
    gate_blocks,
    gate_scales,
    up_blocks,
    up_scales,
    down_blocks,
    down_scales,
    first_stored,
    second_stored,
    owner_map,
):
    group = lax.axis_index("groups")
    half_id = lax.axis_index("dp")
    group_count = lax.axis_size("groups")
    dp_count = lax.axis_size("dp")
    owners = lax.axis_size("tensor") * dp_count
    paired = group_count % 2 == 0
    ff, width = first_stored.shape
    rows = ff // owners
    side = lax.rem(group, 2)

    own_kernels = dp_count == 2 and owners <= 16 and owners % 8 == 0 and inputs.shape[0] % 16 == 0
    if own_kernels:
        x_all, cot = gather_tokens(inputs, cotangent)
    else:
        x_all = lax.all_gather(inputs, TOKENS_AXES, axis=0, tiled=True)
        cot = lax.all_gather(cotangent, TOKENS_AXES, axis=0, tiled=True)

    unit = rows // sum(SHARES)
    shares = SHARES if unit % 16 == 0 and unit else (1,)
    step = rows // sum(shares)
    bounds = []
    for share in shares:
        start = bounds[-1][1] if bounds else 0
        bounds.append((start, start + share * step))
    units = gate_blocks.shape[1] // dp_count
    tiles = units // BLOCK
    cut = lambda a, size, dim: lax.dynamic_slice_in_dim(a, half_id * size, size, dim)
    w_gate = dequantize(cut(gate_blocks, units, 1), cut(gate_scales, tiles, 1), BLOCK)
    shaped_first = first_stored.reshape(owners, rows, width)
    shaped_second = second_stored.reshape(owners, rows, width)
    swap = [(i, i ^ 1) for i in range(group_count)]
    received = []
    for c, (start, stop) in enumerate(bounds):
        if c == 1:
            shaped_first, shaped_second, w_gate = lax.optimization_barrier(
                (shaped_first, shaped_second, w_gate)
            )
        pieces = (shaped_first[:, start:stop], shaped_second[:, start:stop])
        if paired:
            picked = jnp.where(side == 0, *pieces)
            if c == 0:
                picked, x_all, cot = lax.optimization_barrier((picked, x_all, cot))
            mine = lax.all_to_all(picked, TOKENS_AXES, split_axis=0, concat_axis=0, tiled=True)
            other = lax.ppermute(mine, "groups", swap)
            received.append((mine, other))
        else:
            received.append(
                tuple(
                    lax.all_to_all(a, TOKENS_AXES, split_axis=0, concat_axis=0, tiled=True)
                    for a in pieces
                )
            )

    w_up = dequantize(cut(up_blocks, units, 1), cut(up_scales, tiles, 1), BLOCK)
    w_down = dequantize(cut(down_blocks, units, 0), cut(down_scales, tiles, 0), BLOCK)

    gate_pre = jnp.dot(x_all, w_gate, preferred_element_type=jnp.float32)
    up_pre = jnp.dot(x_all, w_up, preferred_element_type=jnp.float32)
    activated, slope = silu_parts(gate_pre)
    hidden = (activated * up_pre).astype(jnp.bfloat16)
    back_hidden = lax.dot_general(
        cot, w_down, (((1,), (1,)), ((), ())), preferred_element_type=jnp.float32
    )
    grad_gate = (back_hidden * up_pre * slope).astype(jnp.bfloat16)
    grad_up = (back_hidden * activated).astype(jnp.bfloat16)
    nt = (((1,), (1,)), ((), ()))
    partial = lax.dot_general(grad_gate, w_gate, nt, preferred_element_type=jnp.float32)
    partial = partial + lax.dot_general(grad_up, w_up, nt, preferred_element_type=jnp.float32)
    partial = partial.astype(jnp.bfloat16)
    if own_kernels:
        input_grad = scatter_sum(partial)
    else:
        input_grad = lax.psum_scatter(partial, TOKENS_AXES, scatter_dimension=0, tiled=True)

    grad = lax.dot_general(
        hidden, cot, (((0,), (0,)), ((), ())), preferred_element_type=jnp.float32
    )
    grad = grad / cot.shape[0]
    if width % 128 == 0 and step % 16 == 0:
        sides = jnp.full((1,), side if paired else 0, jnp.int32)
        update = None
        for c, (mine, other) in enumerate(received):
            update = adam_chunk(
                bounds[c][0], step, owner_map, sides, grad, mine, other, update
            )
    else:
        placement = jnp.zeros((owners,), jnp.int32).at[owner_map].set(
            jnp.arange(owners, dtype=jnp.int32)
        )
        parts = []
        for c, (mine, other) in enumerate(received):
            if paired:
                first = jnp.where(side == 0, mine, other)
                second = jnp.where(side == 0, other, mine)
            else:
                first, second = mine, other
            start, stop = bounds[c]
            lay = lambda a: jnp.take(a, placement, axis=0).swapaxes(0, 1).reshape(stop - start, -1)
            parts.append(adam(lay(first), lay(second), grad[start:stop]))
        update = jnp.concatenate(parts, axis=0)
    return (input_grad, update)


def solution(mesh):
    return step_on(mesh)


def step_on(mesh):
    return jax.shard_map(
        step_of,
        mesh=mesh,
        in_specs=(
            P(("groups", "tensor", "dp"), None),
            P(("groups", "tensor", "dp"), None),
            P(None, "tensor"),
            P(None, "tensor"),
            P(None, "tensor"),
            P(None, "tensor"),
            P("tensor", None),
            P("tensor", None),
            P(None, ("tensor", "dp")),
            P(None, ("tensor", "dp")),
            P(),
        ),
        out_specs=(P(("groups", "tensor", "dp"), None), P(("groups", "tensor", "dp"), None)),
        check_vma=False,
    )
```
